256 devices in a mesh: seq: 32 (over z, x), tp: 8 (over y, core).
Axes of the slice: x: 4, y: 4, z: 8, core: 2. Of those that a mesh axis runs over, the one named last changes fastest.
Arguments:
- tokens_in: bfloat16 [8, 4, 2560], P(None, None, 'tp'), may hold values from -32 to 32
- attn_gain: bfloat16 [2560], replicated, may hold values from 0.25 to 1.75
- mlp_gain: bfloat16 [2560], replicated, may hold values from 0.25 to 1.75
- proj_query: bfloat16 [2560, 2560], P(None, 'tp'), may hold values from -0.125 to 0.125
- proj_key: bfloat16 [2560, 640], P(None, 'tp'), may hold values from -0.125 to 0.125
- proj_value: bfloat16 [2560, 640], P(None, 'tp'), may hold values from -0.125 to 0.125
- proj_out: bfloat16 [2560, 2560], P('tp'), may hold values from -0.125 to 0.125
- proj_gate: bfloat16 [2560, 3456], P(None, 'tp'), may hold values from -0.125 to 0.125
- proj_up: bfloat16 [2560, 3456], P(None, 'tp'), may hold values from -0.125 to 0.125
- proj_down: bfloat16 [3456, 2560], P('tp'), may hold values from -0.109375 to 0.109375
- long_keys: bfloat16 [4096, 8, 80], P('seq', 'tp'), may hold values from -340 to 340
- long_values: bfloat16 [4096, 8, 80], P('seq', 'tp'), may hold values from -6 to 6
- short_keys: bfloat16 [512, 8, 240], P('seq', 'tp'), may hold values from -340 to 340
- short_values: bfloat16 [512, 8, 240], P('seq', 'tp'), may hold values from -6 to 6
- long_seen: int32 [1], replicated, may hold values from 4096 to 8191
- short_len: int32 [3], replicated, may hold values from 1 to 504, as said below
Outputs:
- layer_out: bfloat16 [8, 4, 2560], P(None, None, 'tp')
The draws below stay inside these ranges and needn't reach their ends.
Inputs may be any that keep to these rules, and one draw needn't show every extreme that they name: `short_len`: some short request has exactly 504 cached tokens and some exactly 1.
All inputs are finite; a program needn't handle non-finite values.
Results may differ from the reference program's by a relative error of at most 0.01.
Values may be sent and summed in bfloat16 or wider, within the bound.
No kernel may reach another device: no remote copies, remote signals or barrier semaphores. Data moves between devices by JAX's collectives and lax.ppermute only.
A program may use at most 128 MiB of HBM per device.

```python
import math
import jax
import jax.numpy as jnp
from jax import lax

D = 2560
HEADS = 32
KV_HEADS = 8
HD = 80
FF = 3456
WIN = 4096
SCAP = 512
STEPS = 8
LONG = 1
SHORT = 3


def draw_tokens_in(key, part):
    total_reqs = LONG + SHORT
    key_base, key_cols, key_rows = jax.random.split(jax.random.fold_in(key, 17), 3)
    col_ramp = 0.5 + jnp.arange(D, dtype=jnp.float32) / D
    col_scale = 10.0 ** (jax.random.uniform(key_cols, (D,), dtype=jnp.float32) - 0.5) * col_ramp
    base_draw = jax.random.truncated_normal(key_base, -4.0, 4.0, (STEPS, total_reqs, D), dtype=jnp.float32)
    row_scale = 10.0 ** (jax.random.uniform(key_rows, (STEPS, total_reqs, 1), dtype=jnp.float32) * 0.4 - 0.2)
    return (base_draw * col_scale * row_scale).astype(jnp.bfloat16)


def cache_key_draw(key, slots, requests):
    key_base = jax.random.fold_in(key, 0)
    base_draw = 2.0 * jax.random.truncated_normal(key_base, -3.0, 3.0, (slots, KV_HEADS, requests, HD), dtype=jnp.float32)
    return base_draw.reshape(slots, KV_HEADS, requests * HD).astype(jnp.bfloat16)


def draw_long_keys(key, part):
    return cache_key_draw(jax.random.fold_in(key, 23), WIN, LONG)


def draw_short_keys(key, part):
    return cache_key_draw(jax.random.fold_in(key, 29), SCAP, SHORT)


def draw_short_len(key, part):
    key_len, key_pick = jax.random.split(jax.random.fold_in(key, 41), 2)
    lengths = jax.random.randint(key_len, (SHORT,), 1, SCAP - STEPS + 1)
    pick_index = jax.random.randint(key_pick, (), 0, SHORT)
    slot_ids = jnp.arange(SHORT, dtype=jnp.int32)
    lengths = jnp.where(slot_ids == pick_index, SCAP - STEPS, lengths)
    lengths = jnp.where(slot_ids == (pick_index + 1) % SHORT, 1, lengths)
    return lengths.astype(jnp.int32)


def levels(key, dims, cuts, least, high):
    def one(dim, shards_of):
        draws = jax.random.uniform(jax.random.fold_in(jax.random.fold_in(key, 6), dim), (shards_of,), jnp.float32, least / len(cuts), high / len(cuts))
        return jnp.repeat(jnp.exp(draws), dims[dim] // shards_of).reshape((-1,) + (1,) * (len(dims) - dim - 1))

    factor_of = one(*cuts[0])
    for cut in cuts[1:]:
        factor_of = factor_of * one(*cut)
    return factor_of


def centred(stream_key, extent, scale, limit, pieces=(), kind=jnp.bfloat16):
    drawn = scale * jax.random.normal(stream_key, extent, jnp.float32)
    if pieces:
        drawn = drawn * levels(stream_key, extent, pieces, -0.22, 0.18)
    return jnp.clip(drawn, -limit, limit).astype(kind)


def setup_inputs(seed: int = 0) -> dict:
    arg_keys = jax.random.split(jax.random.key(seed), 17)
    return {
        "tokens_in": draw_tokens_in(jax.random.fold_in(arg_keys[16], 71), 0),
        "attn_gain": jnp.clip(1.0 + 0.15 * jax.random.normal(arg_keys[1], (D,), jnp.float32), 0.25, 1.75).astype(jnp.bfloat16),
        "mlp_gain": jnp.clip(1.0 + 0.15 * jax.random.normal(arg_keys[2], (D,), jnp.float32), 0.25, 1.75).astype(jnp.bfloat16),
        "proj_query": centred(arg_keys[3], (D, HEADS * HD), D ** -0.5, 0.125, ((1, 8),)),
        "proj_key": centred(arg_keys[4], (D, KV_HEADS * HD), D ** -0.5, 0.125, ((1, 8),)),
        "proj_value": centred(arg_keys[5], (D, KV_HEADS * HD), D ** -0.5, 0.125, ((1, 8),)),
        "proj_out": centred(arg_keys[6], (HEADS * HD, D), (HEADS * HD) ** -0.5, 0.125, ((0, 8),)),
        "proj_gate": centred(arg_keys[7], (D, FF), D ** -0.5, 0.125, ((1, 8),)),
        "proj_up": centred(arg_keys[8], (D, FF), D ** -0.5, 0.125, ((1, 8),)),
        "proj_down": centred(arg_keys[9], (FF, D), FF ** -0.5, 0.109375, ((0, 8),)),
        "long_keys": draw_long_keys(jax.random.fold_in(arg_keys[16], 71), 0),
        "long_values": centred(arg_keys[11], (WIN, KV_HEADS, LONG * HD), 2.0, 6.0, ((0, 32), (1, 8))),
        "short_keys": draw_short_keys(jax.random.fold_in(arg_keys[16], 71), 0),
        "short_values": centred(arg_keys[13], (SCAP, KV_HEADS, SHORT * HD), 2.0, 6.0, ((0, 32), (1, 8))),
        "long_seen": jax.random.randint(arg_keys[14], (LONG,), WIN, 2 * WIN).astype(jnp.int32),
        "short_len": draw_short_len(jax.random.fold_in(arg_keys[16], 71), 0),
    }


eps_norm = 1e-05
theta_base = 10000.0
masked_score = -1e+30

def rms_scaled(hidden_rows, norm_gain):
    mean_square = lax.optimization_barrier(jnp.mean(hidden_rows * hidden_rows, axis=-1, keepdims=True))
    return hidden_rows * lax.rsqrt(mean_square + eps_norm) * norm_gain.astype(jnp.float32)

def rotate(vectors, positions):
    half_width = vectors.shape[-1] // 2
    freq_index = jnp.arange(half_width, dtype=jnp.float32)
    frequency = theta_base ** (-2.0 * freq_index / vectors.shape[-1])
    angles = positions.astype(jnp.float32)[..., None] * frequency
    view_shape = angles.shape[:2] + (1,) * (vectors.ndim - 3) + (half_width,)
    cosine_table = jnp.cos(angles).reshape(view_shape)
    sine_table = jnp.sin(angles).reshape(view_shape)
    front_part = vectors[..., :half_width]
    back_part = vectors[..., half_width:]
    return jnp.concatenate([front_part * cosine_table - back_part * sine_table, back_part * cosine_table + front_part * sine_table], axis=-1)

def round_weights(weights):
    return lax.optimization_barrier(weights.astype(jnp.bfloat16)).astype(jnp.float32)

def attend(queries, cache_keys, cache_values, cache_valid, fresh_keys, fresh_values, fresh_valid):
    score_scale = 1.0 / math.sqrt(queries.shape[-1])
    query_float = queries.astype(jnp.float32)
    old_scores = jnp.einsum('trkgd,wkrd->trkgw', query_float, cache_keys.astype(jnp.float32)) * score_scale
    new_scores = jnp.einsum('trkgd,wkrd->trkgw', query_float, fresh_keys.astype(jnp.float32)) * score_scale
    old_mask = cache_valid[:, :, None, None, :]
    new_mask = fresh_valid[:, :, None, None, :]
    old_scores = jnp.where(old_mask, old_scores, masked_score)
    new_scores = jnp.where(new_mask, new_scores, masked_score)
    row_top = jnp.maximum(lax.optimization_barrier(jnp.max(old_scores, axis=-1)), lax.optimization_barrier(jnp.max(new_scores, axis=-1)))[..., None]
    old_weights = jnp.where(old_mask, jnp.exp(old_scores - row_top), 0.0)
    new_weights = jnp.where(new_mask, jnp.exp(new_scores - row_top), 0.0)
    weight_sum = lax.optimization_barrier(jnp.sum(old_weights, axis=-1)) + lax.optimization_barrier(jnp.sum(new_weights, axis=-1))
    weighted = jnp.einsum('trkgw,wkrd->trkgd', round_weights(old_weights), cache_values.astype(jnp.float32))
    weighted = weighted + jnp.einsum('trkgw,wkrd->trkgd', round_weights(new_weights), fresh_values.astype(jnp.float32))
    return weighted / weight_sum[..., None]

def reference(tokens_in, attn_gain, mlp_gain, proj_query, proj_key, proj_value, proj_out, proj_gate, proj_up, proj_down, long_keys, long_values, short_keys, short_values, long_seen, short_len):
    total_reqs = LONG + SHORT
    group_size = HEADS // KV_HEADS
    step_ids = jnp.arange(STEPS, dtype=jnp.int32)
    base_pos = jnp.concatenate([long_seen, short_len]).astype(jnp.int32)
    positions = step_ids[:, None] + base_pos[None, :]
    rows_in = tokens_in.astype(jnp.float32)
    normed = rms_scaled(rows_in, attn_gain).astype(jnp.bfloat16)
    flat_rows = normed.reshape(STEPS * total_reqs, D)
    queries = jnp.dot(flat_rows, proj_query, preferred_element_type=jnp.float32)
    queries = rotate(queries.reshape(STEPS, total_reqs, KV_HEADS, group_size, HD), positions).astype(jnp.bfloat16)
    new_keys = jnp.dot(flat_rows, proj_key, preferred_element_type=jnp.float32)
    new_keys = rotate(new_keys.reshape(STEPS, total_reqs, KV_HEADS, HD), positions).astype(jnp.bfloat16)
    new_keys = new_keys.transpose(0, 2, 1, 3)
    new_values = jnp.dot(flat_rows, proj_value, preferred_element_type=jnp.float32)
    new_values = new_values.reshape(STEPS, total_reqs, KV_HEADS, HD).astype(jnp.bfloat16).transpose(0, 2, 1, 3)
    fresh_valid = jnp.broadcast_to(step_ids[None, None, :] <= step_ids[:, None, None], (STEPS, total_reqs, STEPS))
    long_age = (jnp.arange(WIN, dtype=jnp.int32)[None, :] - (long_seen % WIN)[:, None]) % WIN
    long_valid = long_age[None, :, :] > step_ids[:, None, None]
    short_live = jnp.arange(SCAP, dtype=jnp.int32)[None, :] < short_len[:, None]
    short_valid = jnp.broadcast_to(short_live[None], (STEPS, SHORT, SCAP))
    long_out = attend(queries[:, :LONG], long_keys.reshape(WIN, KV_HEADS, LONG, HD), long_values.reshape(WIN, KV_HEADS, LONG, HD), long_valid, new_keys[:, :, :LONG], new_values[:, :, :LONG], fresh_valid[:, :LONG])
    short_out = attend(queries[:, LONG:], short_keys.reshape(SCAP, KV_HEADS, SHORT, HD), short_values.reshape(SCAP, KV_HEADS, SHORT, HD), short_valid, new_keys[:, :, LONG:], new_values[:, :, LONG:], fresh_valid[:, LONG:])
    attended = jnp.concatenate([long_out, short_out], axis=1).astype(jnp.bfloat16)
    attended = attended.reshape(STEPS * total_reqs, HEADS * HD)
    stream = rows_in + jnp.dot(attended, proj_out, preferred_element_type=jnp.float32).reshape(STEPS, total_reqs, D)
    mlp_in = rms_scaled(stream, mlp_gain).astype(jnp.bfloat16).reshape(STEPS * total_reqs, D)
    gate_act = jnp.dot(mlp_in, proj_gate, preferred_element_type=jnp.float32)
    up_act = jnp.dot(mlp_in, proj_up, preferred_element_type=jnp.float32)
    hidden_act = (jax.nn.silu(gate_act) * up_act).astype(jnp.bfloat16)
    down_act = jnp.dot(hidden_act, proj_down, preferred_element_type=jnp.float32).reshape(STEPS, total_reqs, D)
    return (stream + down_act).astype(jnp.bfloat16)
```

```python
import math

import jax
import jax.numpy as jnp
import numpy as np
from jax import lax
from jax.experimental import pallas as pl
from jax.experimental.pallas import tpu as pltpu
from jax.sharding import Mesh, PartitionSpec as P

HEADS = 32
KV_HEADS = 8
GROUP = HEADS // KV_HEADS
HD = 80
HALF = HD // 2
D = 2560
WIN = 4096
STEPS = 8
REQS = 4
ROWS = STEPS * REQS
NZ, NX, NY, NC = 8, 4, 4, 2
NSEQ = NZ * NX
NTP = NY * NC
LOCAL = D // NTP
SLOTS = WIN // NSEQ
SSLOTS = 16
EPS = 1e-05
MASKED = -1e30
SEQ = ("z", "x")
TP = ("y", "c")
F32 = jnp.float32
BF16 = jnp.bfloat16
NN = (((1,), (0,)), ((), ()))
NT = (((1,), (1,)), ((), ()))
TN = (((0,), (0,)), ((), ()))


def mm(a, b, dims):
    return lax.dot_general(a, b, dims, preferred_element_type=F32)


def iota(shape, dim):
    return lax.broadcasted_iota(jnp.int32, shape, dim)


def wide_rows(piece):
    return jnp.concatenate([piece(c) for c in range(NTP)], axis=-1)


def split3(v):
    hi = v.astype(BF16).astype(F32)
    mid = (v - hi).astype(BF16).astype(F32)
    low = (v - hi - mid).astype(BF16).astype(F32)
    return hi, mid, low


def attend_kernel(
    seen_ref, len_ref, x_ref, gain_ref, freq_ref, wq_ref, wk_ref, wv_ref,
    lk_ref, lv_ref, sk_ref, sv_ref, part_ref, own_ref,
):
    z_rank = lax.axis_index("z")
    seq_rank = z_rank * NX + lax.axis_index("x")
    x_bf = wide_rows(lambda c: x_ref[c])
    x = x_bf.astype(F32)
    mean_square = jnp.mean(x * x, axis=-1, keepdims=True)
    normed = (x * lax.rsqrt(mean_square + EPS) * gain_ref[...].astype(F32)).astype(BF16)
    pick = (iota((8, ROWS), 1) == z_rank * REQS + iota((8, ROWS), 0)).astype(BF16)
    own_ref[...] = mm(pick, x_bf, NN)[:REQS]

    col = iota((HALF, ROWS), 1)
    req = col & 3
    base = jnp.where(req == 0, seen_ref[0], jnp.where(req == 1, len_ref[0], jnp.where(req == 2, len_ref[1], len_ref[2])))
    angles = ((col >> 2) + base).astype(F32) * freq_ref[...]
    cos = jnp.cos(angles)
    sin = jnp.sin(angles)

    def rope(v):
        front, back = v[:HALF], v[HALF:]
        return jnp.concatenate([front * cos - back * sin, back * cos + front * sin], axis=0)

    q_t = mm(wq_ref[...], normed, NT)
    k_t = rope(mm(wk_ref[...], normed, NT)).astype(BF16)
    v_t = mm(wv_ref[...], normed, NT).astype(BF16)
    q_all = jnp.concatenate([rope(q_t[h * HD : (h + 1) * HD]) for h in range(GROUP)], axis=1)
    q = q_all.T.astype(BF16)

    scale = 1.0 / math.sqrt(HD)
    n_rows = GROUP * ROWS
    sk = jnp.concatenate([sk_ref[:, r * HD : (r + 1) * HD] for r in range(REQS - 1)], axis=0)
    sv = jnp.concatenate([sv_ref[:, r * HD : (r + 1) * HD] for r in range(REQS - 1)], axis=0)
    s_long = mm(q, lk_ref[...], NN) * scale
    s_short = mm(q, sk, NT) * scale
    s_new = mm(q, k_t, NN) * scale

    def row_ids(shape):
        row = iota(shape, 0)
        return row & 3, (row >> 2) & 7

    r, t = row_ids(s_long.shape)
    age = (seq_rank * SLOTS + iota(s_long.shape, 1) - seen_ref[0]) & (WIN - 1)
    see_long = (r == 0) & (age > t)
    r, t = row_ids(s_short.shape)
    j = iota(s_short.shape, 1)
    n_cached = jnp.where(r == 1, len_ref[0], jnp.where(r == 2, len_ref[1], len_ref[2]))
    see_short = ((j >> 4) + 1 == r) & (seq_rank * SSLOTS + (j & 15) < n_cached)
    r, t = row_ids(s_new.shape)
    j = iota(s_new.shape, 1)
    see_new = ((j & 3) == r) & ((j >> 2) <= t) & (seq_rank == 0)
    s_long = jnp.where(see_long, s_long, MASKED)
    s_short = jnp.where(see_short, s_short, MASKED)
    s_new = jnp.where(see_new, s_new, MASKED)
    top = jnp.maximum(
        jnp.maximum(jnp.max(s_long, axis=-1, keepdims=True), jnp.max(s_short, axis=-1, keepdims=True)),
        jnp.max(s_new, axis=-1, keepdims=True),
    )
    w_long = jnp.where(see_long, jnp.exp(s_long - top), 0.0)
    w_short = jnp.where(see_short, jnp.exp(s_short - top), 0.0)
    w_new = jnp.where(see_new, jnp.exp(s_new - top), 0.0)
    total = (
        jnp.sum(w_long, axis=-1, keepdims=True)
        + jnp.sum(w_short, axis=-1, keepdims=True)
        + jnp.sum(w_new, axis=-1, keepdims=True)
    )
    acc = (
        mm(w_long.astype(BF16), lv_ref[...], NT)
        + mm(w_short.astype(BF16), sv, NN)
        + mm(w_new.astype(BF16), v_t, NT)
    )
    top_a, top_b, top_c = split3(top)
    sum_a, sum_b, _ = split3(total)
    acc = jnp.concatenate([acc, jnp.zeros((n_rows, 128 - HD), F32)], axis=1)
    lane = iota(acc.shape, 1)
    for k, v in enumerate((top_a, top_b, top_c, sum_a, sum_b)):
        acc = jnp.where(lane == HD + k, v, acc)
    for step in range(STEPS):
        rows = jnp.concatenate(
            [acc[h * ROWS + step * REQS : h * ROWS + (step + 1) * REQS] for h in range(GROUP)], axis=0
        ).astype(BF16)
        for x_to in range(NX):
            part_ref[step * NX + x_to] = rows


def combine_kernel(part_ref, wo_ref, out_ref):
    part = part_ref[...]
    src = iota((128, 256), 0)
    dst = iota((128, 256), 1)
    spread = (
        ((dst < 128) & (src >= HD) & (src < HD + 3)) | ((dst >= 128) & (src >= HD + 3) & (src < HD + 5))
    ).astype(BF16)
    stats = mm(part.reshape(NSEQ * 16, 128), spread, NN)
    top = stats[:, :128].reshape(NSEQ, 16, 128)
    total = stats[:, 128:].reshape(NSEQ, 16, 128)
    factor = jnp.exp(top - jnp.max(top, axis=0, keepdims=True))
    weighted = jnp.sum(part.astype(F32) * factor, axis=0)
    attended = weighted / jnp.sum(total * factor, axis=0)
    attended = jnp.concatenate([attended[h * REQS : (h + 1) * REQS, :HD] for h in range(GROUP)], axis=1)
    term = mm(attended.astype(BF16), wo_ref[...], NN).astype(BF16)
    for to in range(NTP):
        out_ref[to] = term


def mlp_kernel(part_ref, own_ref, gain_ref, wg_ref, wu_ref, wd_ref, out_ref):
    tp_rank = lax.axis_index("y") * NC + lax.axis_index("c")
    head_sum = jnp.sum(part_ref[...].astype(F32), axis=0)
    stream = own_ref[...] + head_sum
    mean_square = jnp.mean(stream * stream, axis=-1, keepdims=True)
    mlp_in = stream * lax.rsqrt(mean_square + EPS) * gain_ref[...].astype(F32)
    mlp_in = jnp.concatenate([mlp_in, jnp.zeros((16 - REQS, D), F32)], axis=0).astype(BF16)
    gate = mm(wg_ref[...], mlp_in, NT)
    up = mm(wu_ref[...], mlp_in, NT)
    hidden = (gate / (1.0 + jnp.exp(-gate)) * up).astype(BF16)
    down = mm(hidden, wd_ref[...], TN)[:REQS]
    for to in range(NTP):
        cols = slice(to * LOCAL, (to + 1) * LOCAL)
        piece = (down[:, cols] + jnp.where(tp_rank == to, head_sum[:, cols], 0.0)).astype(BF16)
        for z_to in range(NZ):
            out_ref[z_to * NTP + to] = piece


def call(kernel, out_shape, n_smem, args):
    specs = [pl.BlockSpec(memory_space=pltpu.SMEM)] * n_smem + [pl.BlockSpec(memory_space=pltpu.VMEM)] * (
        len(args) - n_smem
    )
    return pl.pallas_call(
        kernel,
        out_shape=out_shape,
        in_specs=specs,
        compiler_params=pltpu.CompilerParams(vmem_limit_bytes=24 * 1024 * 1024),
    )(*args)


def body(
    tokens_in, attn_gain, mlp_gain, proj_query, proj_key, proj_value, proj_out, proj_gate, proj_up,
    proj_down, long_keys, long_values, short_keys, short_values, long_seen, short_len,
):
    freq = 10000.0 ** (-2.0 * np.arange(HALF) / HD)
    freq = jnp.asarray(np.repeat(freq[:, None], ROWS, axis=1).astype(np.float32))
    flat = tokens_in.reshape(ROWS, LOCAL)
    x_all = lax.all_to_all(jnp.broadcast_to(flat[None], (NTP, ROWS, LOCAL)), TP, 0, 0, tiled=True)
    parts, own = call(
        attend_kernel,
        (jax.ShapeDtypeStruct((NSEQ, 16, 128), BF16), jax.ShapeDtypeStruct((REQS, D), F32)),
        2,
        (
            long_seen, short_len, x_all, attn_gain.reshape(1, D), freq,
            proj_query.T, proj_key.T, proj_value.T,
            long_keys.reshape(SLOTS, HD).T, long_values.reshape(SLOTS, HD).T,
            short_keys.reshape(SSLOTS, 3 * HD), short_values.reshape(SSLOTS, 3 * HD),
        ),
    )
    parts = lax.all_to_all(parts, SEQ, 0, 0, tiled=True)
    terms = call(combine_kernel, jax.ShapeDtypeStruct((NTP, REQS, D), BF16), 0, (parts, proj_out))
    terms = lax.all_to_all(terms, TP, 0, 0, tiled=True)
    pieces = call(
        mlp_kernel,
        jax.ShapeDtypeStruct((NZ * NTP, REQS, LOCAL), BF16),
        0,
        (terms, own, mlp_gain.reshape(1, D), proj_gate.T, proj_up.T, proj_down),
    )
    pieces = lax.all_to_all(pieces, ("z",) + TP, 0, 0, tiled=True)
    total = jnp.sum(pieces.reshape(NZ, NTP, REQS, LOCAL).astype(F32), axis=1)
    return (tokens_in.astype(F32) + total).astype(BF16)


def solution(mesh):
    fine = Mesh(mesh.devices.reshape(NZ, NX, NY, NC), ("z", "x", "y", "c"))
    cols = P(None, TP)
    rows = P(TP, None)
    cache = P(SEQ, TP, None)
    in_specs = (
        P(None, None, TP), P(), P(), cols, cols, cols, rows, cols, cols, rows,
        cache, cache, cache, cache, P(), P(),
    )
    return jax.shard_map(body, mesh=fine, in_specs=in_specs, out_specs=P(None, None, TP), check_vma=False)
```

```python
import math

import jax
import jax.numpy as jnp
import numpy as np
from jax import lax
from jax.experimental import pallas as pl
from jax.experimental.pallas import tpu as pltpu
from jax.sharding import Mesh, PartitionSpec as P

HEADS = 32
KV_HEADS = 8
GROUP = HEADS // KV_HEADS
HD = 80
HALF = HD // 2
D = 2560
WIN = 4096
STEPS = 8
REQS = 4
ROWS = STEPS * REQS
NZ, NX, NY, NC = 8, 4, 4, 2
NSEQ = NZ * NX
NTP = NY * NC
LOCAL = D // NTP
SLOTS = WIN // NSEQ
SSLOTS = 16
EPS = 1e-05
MASKED = -1e30
SEQ = ("z", "x")
TP = ("y", "c")
F32 = jnp.float32
BF16 = jnp.bfloat16
NN = (((1,), (0,)), ((), ()))
NT = (((1,), (1,)), ((), ()))
TN = (((0,), (0,)), ((), ()))


def mm(a, b, dims):
    return lax.dot_general(a, b, dims, preferred_element_type=F32)


def iota(shape, dim):
    return lax.broadcasted_iota(jnp.int32, shape, dim)


def wide_rows(piece):
    return jnp.concatenate([piece(c) for c in range(NTP)], axis=-1)


def split3(v):
    hi = v.astype(BF16).astype(F32)
    mid = (v - hi).astype(BF16).astype(F32)
    low = (v - hi - mid).astype(BF16).astype(F32)
    return hi, mid, low


def spread_kernel(tokens_ref, out_ref):
    rows = jnp.concatenate([tokens_ref[t].astype(F32) for t in range(STEPS)], axis=0).astype(BF16)
    for to in range(NTP):
        out_ref[to] = rows


def finish_kernel(piece_ref, tokens_ref, out_ref):
    for z_from in range(NZ):
        total = jnp.sum(piece_ref[z_from * NTP : (z_from + 1) * NTP].astype(F32), axis=0)
        out_ref[z_from] = (tokens_ref[z_from].astype(F32) + total).astype(BF16)


def attend_kernel(
    seen_hbm, len_hbm, x_ref, gain_ref, freq_ref, wq_ref, wk_ref, wv_ref,
    lk_ref, lv_ref, sk_ref, sv_ref, part_ref, own_ref, seen_ref, len_ref, sems,
):
    loads = [pltpu.make_async_copy(seen_hbm, seen_ref, sems.at[0]), pltpu.make_async_copy(len_hbm, len_ref, sems.at[1])]
    for load in loads:
        load.start()
    z_rank = lax.axis_index("z")
    seq_rank = z_rank * NX + lax.axis_index("x")
    x_bf = wide_rows(lambda c: x_ref[c])
    x = x_bf.astype(F32)
    mean_square = jnp.mean(x * x, axis=-1, keepdims=True)
    normed = (x * lax.rsqrt(mean_square + EPS) * gain_ref[...].astype(F32).reshape(1, D)).astype(BF16)
    pick = (iota((8, ROWS), 1) == z_rank * REQS + iota((8, ROWS), 0)).astype(BF16)
    own_ref[...] = mm(pick, x_bf, NN)[:REQS]

    for load in loads:
        load.wait()
    col = iota((HALF, ROWS), 1)
    req = col & 3
    base = jnp.where(req == 0, seen_ref[0], jnp.where(req == 1, len_ref[0], jnp.where(req == 2, len_ref[1], len_ref[2])))
    angles = ((col >> 2) + base).astype(F32) * freq_ref[...]
    cos = jnp.cos(angles)
    sin = jnp.sin(angles)

    def rope(v):
        front, back = v[:HALF], v[HALF:]
        return jnp.concatenate([front * cos - back * sin, back * cos + front * sin], axis=0)

    q_t = mm(wq_ref[...], normed, NT)
    k_t = rope(mm(wk_ref[...], normed, NT)).astype(BF16)
    v_t = mm(wv_ref[...], normed, NT).astype(BF16)
    q_all = jnp.concatenate([rope(q_t[h * HD : (h + 1) * HD]) for h in range(GROUP)], axis=1)
    q = q_all.T.astype(BF16)

    scale = 1.0 / math.sqrt(HD)
    n_rows = GROUP * ROWS
    sk = jnp.concatenate([sk_ref[:, r * HD : (r + 1) * HD] for r in range(REQS - 1)], axis=0)
    sv = jnp.concatenate([sv_ref[:, r * HD : (r + 1) * HD] for r in range(REQS - 1)], axis=0)
    s_long = mm(q, lk_ref[...], NN) * scale
    s_short = mm(q, sk, NT) * scale
    s_new = mm(q, k_t, NN) * scale

    def row_ids(shape):
        row = iota(shape, 0)
        return row & 3, (row >> 2) & 7

    r, t = row_ids(s_long.shape)
    age = (seq_rank * SLOTS + iota(s_long.shape, 1) - seen_ref[0]) & (WIN - 1)
    see_long = (r == 0) & (age > t)
    r, t = row_ids(s_short.shape)
    j = iota(s_short.shape, 1)
    n_cached = jnp.where(r == 1, len_ref[0], jnp.where(r == 2, len_ref[1], len_ref[2]))
    see_short = ((j >> 4) + 1 == r) & (seq_rank * SSLOTS + (j & 15) < n_cached)
    r, t = row_ids(s_new.shape)
    j = iota(s_new.shape, 1)
    see_new = ((j & 3) == r) & ((j >> 2) <= t) & (seq_rank == 0)
    s_long = jnp.where(see_long, s_long, MASKED)
    s_short = jnp.where(see_short, s_short, MASKED)
    s_new = jnp.where(see_new, s_new, MASKED)
    top = jnp.maximum(
        jnp.maximum(jnp.max(s_long, axis=-1, keepdims=True), jnp.max(s_short, axis=-1, keepdims=True)),
        jnp.max(s_new, axis=-1, keepdims=True),
    )
    w_long = jnp.where(see_long, jnp.exp(s_long - top), 0.0)
    w_short = jnp.where(see_short, jnp.exp(s_short - top), 0.0)
    w_new = jnp.where(see_new, jnp.exp(s_new - top), 0.0)
    total = (
        jnp.sum(w_long, axis=-1, keepdims=True)
        + jnp.sum(w_short, axis=-1, keepdims=True)
        + jnp.sum(w_new, axis=-1, keepdims=True)
    )
    acc = (
        mm(w_long.astype(BF16), lv_ref[...], NT)
        + mm(w_short.astype(BF16), sv, NN)
        + mm(w_new.astype(BF16), v_t, NT)
    )
    top_a, top_b, top_c = split3(top)
    sum_a, sum_b, _ = split3(total)
    acc = jnp.concatenate([acc, jnp.zeros((n_rows, 128 - HD), F32)], axis=1)
    lane = iota(acc.shape, 1)
    for k, v in enumerate((top_a, top_b, top_c, sum_a, sum_b)):
        acc = jnp.where(lane == HD + k, v, acc)
    for step in range(STEPS):
        rows = jnp.concatenate(
            [acc[h * ROWS + step * REQS : h * ROWS + (step + 1) * REQS] for h in range(GROUP)], axis=0
        ).astype(BF16)
        for x_to in range(NX):
            part_ref[step * NX + x_to] = rows


def combine_kernel(part_ref, wo_ref, out_ref):
    part = part_ref[...]
    src = iota((128, 256), 0)
    dst = iota((128, 256), 1)
    spread = (
        ((dst < 128) & (src >= HD) & (src < HD + 3)) | ((dst >= 128) & (src >= HD + 3) & (src < HD + 5))
    ).astype(BF16)
    stats = mm(part.reshape(NSEQ * 16, 128), spread, NN)
    top = stats[:, :128].reshape(NSEQ, 16, 128)
    total = stats[:, 128:].reshape(NSEQ, 16, 128)
    factor = jnp.exp(top - jnp.max(top, axis=0, keepdims=True))
    weighted = jnp.sum(part.astype(F32) * factor, axis=0)
    attended = weighted / jnp.sum(total * factor, axis=0)
    attended = jnp.concatenate([attended[h * REQS : (h + 1) * REQS, :HD] for h in range(GROUP)], axis=1)
    term = mm(attended.astype(BF16), wo_ref[...], NN).astype(BF16)
    for to in range(NTP):
        out_ref[to] = term


def mlp_kernel(part_ref, own_ref, gain_ref, wg_ref, wu_ref, wd_ref, out_ref):
    tp_rank = lax.axis_index("y") * NC + lax.axis_index("c")
    head_sum = jnp.sum(part_ref[...].astype(F32), axis=0)
    stream = own_ref[...] + head_sum
    mean_square = jnp.mean(stream * stream, axis=-1, keepdims=True)
    mlp_in = stream * lax.rsqrt(mean_square + EPS) * gain_ref[...].astype(F32).reshape(1, D)
    mlp_in = jnp.concatenate([mlp_in, jnp.zeros((16 - REQS, D), F32)], axis=0).astype(BF16)
    gate = mm(wg_ref[...], mlp_in, NT)
    up = mm(wu_ref[...], mlp_in, NT)
    hidden = (gate / (1.0 + jnp.exp(-gate)) * up).astype(BF16)
    down = mm(hidden, wd_ref[...], TN)[:REQS]
    for to in range(NTP):
        cols = slice(to * LOCAL, (to + 1) * LOCAL)
        piece = (down[:, cols] + jnp.where(tp_rank == to, head_sum[:, cols], 0.0)).astype(BF16)
        for z_to in range(NZ):
            out_ref[z_to * NTP + to] = piece


def call(kernel, out_shape, n_smem, args, scratch=()):
    specs = [pl.BlockSpec(memory_space=pltpu.HBM)] * n_smem + [pl.BlockSpec(memory_space=pltpu.VMEM)] * (
        len(args) - n_smem
    )
    return pl.pallas_call(
        kernel,
        out_shape=out_shape,
        in_specs=specs,
        scratch_shapes=scratch,
        cost_estimate=pl.CostEstimate(flops=50_000_000_000, bytes_accessed=100_000_000, transcendentals=0),
        compiler_params=pltpu.CompilerParams(vmem_limit_bytes=16 * 1024 * 1024),
    )(*args)


def body(
    tokens_in, attn_gain, mlp_gain, proj_query, proj_key, proj_value, proj_out, proj_gate, proj_up,
    proj_down, long_keys, long_values, short_keys, short_values, long_seen, short_len,
):
    freq = 10000.0 ** (-2.0 * np.arange(HALF) / HD)
    freq = jnp.asarray(np.repeat(freq[:, None], ROWS, axis=1).astype(np.float32))
    copies = call(spread_kernel, jax.ShapeDtypeStruct((NTP, ROWS, LOCAL), BF16), 0, (tokens_in,))
    x_all = lax.all_to_all(copies, TP, 0, 0, tiled=True)
    parts, own = call(
        attend_kernel,
        (jax.ShapeDtypeStruct((NSEQ, 16, 128), BF16), jax.ShapeDtypeStruct((REQS, D), F32)),
        2,
        (
            long_seen, short_len, x_all, attn_gain, freq,
            proj_query.T, proj_key.T, proj_value.T,
            long_keys.reshape(SLOTS, HD).T, long_values.reshape(SLOTS, HD).T,
            short_keys.reshape(SSLOTS, 3 * HD), short_values.reshape(SSLOTS, 3 * HD),
        ),
        (pltpu.SMEM((1,), jnp.int32), pltpu.SMEM((3,), jnp.int32), pltpu.SemaphoreType.DMA((2,))),
    )
    parts = lax.all_to_all(parts, SEQ, 0, 0, tiled=True)
    terms = call(combine_kernel, jax.ShapeDtypeStruct((NTP, REQS, D), BF16), 0, (parts, proj_out))
    terms = lax.all_to_all(terms, TP, 0, 0, tiled=True)
    pieces = call(
        mlp_kernel,
        jax.ShapeDtypeStruct((NZ * NTP, REQS, LOCAL), BF16),
        0,
        (terms, own, mlp_gain, proj_gate.T, proj_up.T, proj_down),
    )
    pieces = lax.all_to_all(pieces, ("z",) + TP, 0, 0, tiled=True)
    return call(finish_kernel, jax.ShapeDtypeStruct((STEPS, REQS, LOCAL), BF16), 0, (pieces, tokens_in))


def solution(mesh):
    fine = Mesh(mesh.devices.reshape(NZ, NX, NY, NC), ("z", "x", "y", "c"))
    cols = P(None, TP)
    rows = P(TP, None)
    cache = P(SEQ, TP, None)
    in_specs = (
        P(None, None, TP), P(), P(), cols, cols, cols, rows, cols, cols, rows,
        cache, cache, cache, cache, P(), P(),
    )
    return jax.shard_map(body, mesh=fine, in_specs=in_specs, out_specs=P(None, None, TP), check_vma=False)
```

```python
import math

import jax
import jax.numpy as jnp
import numpy as np
from jax import lax
from jax.experimental import pallas as pl
from jax.experimental.pallas import tpu as pltpu
from jax.sharding import Mesh, PartitionSpec as P

HEADS = 32
KV_HEADS = 8
GROUP = HEADS // KV_HEADS
HD = 80
HALF = HD // 2
D = 2560
WIN = 4096
STEPS = 8
REQS = 4
ROWS = STEPS * REQS
NH, NL, NX, NY, NC = 4, 2, 4, 4, 2
NZ = NH * NL
NG = NL * NX
NSEQ = NZ * NX
NTP = NY * NC
LOCAL = D // NTP
SLOTS = WIN // NSEQ
SSLOTS = 16
EPS = 1e-05
MASKED = -1e30
SEQ = ("zh", "zl", "x")
TEAM = ("zl", "x")
TP = ("y", "c")
F32 = jnp.float32
BF16 = jnp.bfloat16
NN = (((1,), (0,)), ((), ()))
NT = (((1,), (1,)), ((), ()))
TN = (((0,), (0,)), ((), ()))


def mm(a, b, dims):
    return lax.dot_general(a, b, dims, preferred_element_type=F32)


def iota(shape, dim):
    return lax.broadcasted_iota(jnp.int32, shape, dim)


def wide_rows(piece):
    return jnp.concatenate([piece(c) for c in range(NTP)], axis=-1)


def split3(v):
    hi = v.astype(BF16).astype(F32)
    mid = (v - hi).astype(BF16).astype(F32)
    low = (v - hi - mid).astype(BF16).astype(F32)
    return hi, mid, low


def spread_kernel(tokens_ref, out_ref):
    rows = jnp.concatenate([tokens_ref[t].astype(F32) for t in range(STEPS)], axis=0).astype(BF16)
    for to in range(NTP):
        out_ref[to] = rows


def finish_kernel(piece_ref, tokens_ref, out_ref):
    for step in range(STEPS):
        total = jnp.sum(piece_ref[step * NTP : (step + 1) * NTP].astype(F32), axis=0)
        out_ref[step] = (tokens_ref[step].astype(F32) + total).astype(BF16)


def attend_kernel(
    seen_hbm, len_hbm, x_ref, gain_ref, freq_ref, wq_ref, wk_ref, wv_ref,
    lk_ref, lv_ref, sk_ref, sv_ref, part_ref, own_ref, seen_ref, len_ref, sems,
):
    loads = [pltpu.make_async_copy(seen_hbm, seen_ref, sems.at[0]), pltpu.make_async_copy(len_hbm, len_ref, sems.at[1])]
    for load in loads:
        load.start()
    team_rank = lax.axis_index("zl") * NX + lax.axis_index("x")
    seq_rank = lax.axis_index("zh") * NG + team_rank
    x_bf = wide_rows(lambda c: x_ref[c])
    x = x_bf.astype(F32)
    mean_square = jnp.mean(x * x, axis=-1, keepdims=True)
    normed = (x * lax.rsqrt(mean_square + EPS) * gain_ref[...].astype(F32).reshape(1, D)).astype(BF16)
    pick = (iota((8, ROWS), 1) == team_rank * REQS + iota((8, ROWS), 0)).astype(BF16)
    own_ref[...] = mm(pick, x_bf, NN)[:REQS]

    for load in loads:
        load.wait()
    col = iota((HALF, ROWS), 1)
    req = col & 3
    base = jnp.where(req == 0, seen_ref[0], jnp.where(req == 1, len_ref[0], jnp.where(req == 2, len_ref[1], len_ref[2])))
    angles = ((col >> 2) + base).astype(F32) * freq_ref[...]
    cos = jnp.cos(angles)
    sin = jnp.sin(angles)

    def rope(v):
        front, back = v[:HALF], v[HALF:]
        return jnp.concatenate([front * cos - back * sin, back * cos + front * sin], axis=0)

    q_t = mm(wq_ref[...], normed, NT)
    k_t = rope(mm(wk_ref[...], normed, NT)).astype(BF16)
    v_t = mm(wv_ref[...], normed, NT).astype(BF16)
    q_all = jnp.concatenate([rope(q_t[h * HD : (h + 1) * HD]) for h in range(GROUP)], axis=1)
    q = q_all.T.astype(BF16)

    scale = 1.0 / math.sqrt(HD)
    n_rows = GROUP * ROWS
    sk = jnp.concatenate([sk_ref[:, r * HD : (r + 1) * HD] for r in range(REQS - 1)], axis=0)
    sv = jnp.concatenate([sv_ref[:, r * HD : (r + 1) * HD] for r in range(REQS - 1)], axis=0)
    s_long = mm(q, lk_ref[...], NN) * scale
    s_short = mm(q, sk, NT) * scale
    s_new = mm(q, k_t, NN) * scale

    def row_ids(shape):
        row = iota(shape, 0)
        return row & 3, (row >> 2) & 7

    r, t = row_ids(s_long.shape)
    age = (seq_rank * SLOTS + iota(s_long.shape, 1) - seen_ref[0]) & (WIN - 1)
    see_long = (r == 0) & (age > t)
    r, t = row_ids(s_short.shape)
    j = iota(s_short.shape, 1)
    n_cached = jnp.where(r == 1, len_ref[0], jnp.where(r == 2, len_ref[1], len_ref[2]))
    see_short = ((j >> 4) + 1 == r) & (seq_rank * SSLOTS + (j & 15) < n_cached)
    r, t = row_ids(s_new.shape)
    j = iota(s_new.shape, 1)
    see_new = ((j & 3) == r) & ((j >> 2) <= t) & (seq_rank == 0)
    s_long = jnp.where(see_long, s_long, MASKED)
    s_short = jnp.where(see_short, s_short, MASKED)
    s_new = jnp.where(see_new, s_new, MASKED)
    top = jnp.maximum(
        jnp.maximum(jnp.max(s_long, axis=-1, keepdims=True), jnp.max(s_short, axis=-1, keepdims=True)),
        jnp.max(s_new, axis=-1, keepdims=True),
    )
    w_long = jnp.where(see_long, jnp.exp(s_long - top), 0.0)
    w_short = jnp.where(see_short, jnp.exp(s_short - top), 0.0)
    w_new = jnp.where(see_new, jnp.exp(s_new - top), 0.0)
    total = (
        jnp.sum(w_long, axis=-1, keepdims=True)
        + jnp.sum(w_short, axis=-1, keepdims=True)
        + jnp.sum(w_new, axis=-1, keepdims=True)
    )
    acc = (
        mm(w_long.astype(BF16), lv_ref[...], NT)
        + mm(w_short.astype(BF16), sv, NN)
        + mm(w_new.astype(BF16), v_t, NT)
    )
    top_a, top_b, top_c = split3(top)
    sum_a, sum_b, _ = split3(total)
    acc = jnp.concatenate([acc, jnp.zeros((n_rows, 128 - HD), F32)], axis=1)
    lane = iota(acc.shape, 1)
    for k, v in enumerate((top_a, top_b, top_c, sum_a, sum_b)):
        acc = jnp.where(lane == HD + k, v, acc)
    for step in range(STEPS):
        rows = jnp.concatenate(
            [acc[h * ROWS + step * REQS : h * ROWS + (step + 1) * REQS] for h in range(GROUP)], axis=0
        ).astype(BF16)
        for zh_to in range(NH):
            part_ref[zh_to * NG + step] = rows


def combine_kernel(part_ref, wo_ref, out_ref):
    part = part_ref[...]
    src = iota((128, 256), 0)
    dst = iota((128, 256), 1)
    spread = (
        ((dst < 128) & (src >= HD) & (src < HD + 3)) | ((dst >= 128) & (src >= HD + 3) & (src < HD + 5))
    ).astype(BF16)
    stats = mm(part.reshape(NSEQ * 16, 128), spread, NN)
    top = stats[:, :128].reshape(NSEQ, 16, 128)
    total = stats[:, 128:].reshape(NSEQ, 16, 128)
    factor = jnp.exp(top - jnp.max(top, axis=0, keepdims=True))
    weighted = jnp.sum(part.astype(F32) * factor, axis=0)
    attended = weighted / jnp.sum(total * factor, axis=0)
    attended = jnp.concatenate([attended[h * REQS : (h + 1) * REQS, :HD] for h in range(GROUP)], axis=1)
    term = mm(attended.astype(BF16), wo_ref[...], NN).astype(BF16)
    for to in range(NTP):
        out_ref[to] = term


def mlp_kernel(part_ref, own_ref, gain_ref, wg_ref, wu_ref, wd_ref, out_ref):
    tp_rank = lax.axis_index("y") * NC + lax.axis_index("c")
    head_sum = jnp.sum(part_ref[...].astype(F32), axis=0)
    stream = own_ref[...] + head_sum
    mean_square = jnp.mean(stream * stream, axis=-1, keepdims=True)
    mlp_in = stream * lax.rsqrt(mean_square + EPS) * gain_ref[...].astype(F32).reshape(1, D)
    mlp_in = jnp.concatenate([mlp_in, jnp.zeros((16 - REQS, D), F32)], axis=0).astype(BF16)
    gate = mm(wg_ref[...], mlp_in, NT)
    up = mm(wu_ref[...], mlp_in, NT)
    hidden = (gate / (1.0 + jnp.exp(-gate)) * up).astype(BF16)
    down = mm(hidden, wd_ref[...], TN)[:REQS]
    for to in range(NTP):
        cols = slice(to * LOCAL, (to + 1) * LOCAL)
        piece = (down[:, cols] + jnp.where(tp_rank == to, head_sum[:, cols], 0.0)).astype(BF16)
        for g_to in range(NG):
            out_ref[g_to * NTP + to] = piece


def call(kernel, out_shape, n_smem, args, scratch=()):
    specs = [pl.BlockSpec(memory_space=pltpu.HBM)] * n_smem + [pl.BlockSpec(memory_space=pltpu.VMEM)] * (
        len(args) - n_smem
    )
    return pl.pallas_call(
        kernel,
        out_shape=out_shape,
        in_specs=specs,
        scratch_shapes=scratch,
        cost_estimate=pl.CostEstimate(flops=50_000_000_000, bytes_accessed=100_000_000, transcendentals=0),
        compiler_params=pltpu.CompilerParams(vmem_limit_bytes=16 * 1024 * 1024),
    )(*args)


def body(
    tokens_in, attn_gain, mlp_gain, proj_query, proj_key, proj_value, proj_out, proj_gate, proj_up,
    proj_down, long_keys, long_values, short_keys, short_values, long_seen, short_len,
):
    freq = 10000.0 ** (-2.0 * np.arange(HALF) / HD)
    freq = jnp.asarray(np.repeat(freq[:, None], ROWS, axis=1).astype(np.float32))
    copies = call(spread_kernel, jax.ShapeDtypeStruct((NTP, ROWS, LOCAL), BF16), 0, (tokens_in,))
    x_all = lax.all_to_all(copies, TP, 0, 0, tiled=True)
    parts, own = call(
        attend_kernel,
        (jax.ShapeDtypeStruct((NSEQ, 16, 128), BF16), jax.ShapeDtypeStruct((REQS, D), F32)),
        2,
        (
            long_seen, short_len, x_all, attn_gain, freq,
            proj_query.T, proj_key.T, proj_value.T,
            long_keys.reshape(SLOTS, HD).T, long_values.reshape(SLOTS, HD).T,
            short_keys.reshape(SSLOTS, 3 * HD), short_values.reshape(SSLOTS, 3 * HD),
        ),
        (pltpu.SMEM((1,), jnp.int32), pltpu.SMEM((3,), jnp.int32), pltpu.SemaphoreType.DMA((2,))),
    )
    parts = lax.all_to_all(parts, SEQ, 0, 0, tiled=True)
    terms = call(combine_kernel, jax.ShapeDtypeStruct((NTP, REQS, D), BF16), 0, (parts, proj_out))
    terms = lax.all_to_all(terms, TP, 0, 0, tiled=True)
    pieces = call(
        mlp_kernel,
        jax.ShapeDtypeStruct((NG * NTP, REQS, LOCAL), BF16),
        0,
        (terms, own, mlp_gain, proj_gate.T, proj_up.T, proj_down),
    )
    pieces = lax.all_to_all(pieces, TEAM + TP, 0, 0, tiled=True)
    return call(finish_kernel, jax.ShapeDtypeStruct((STEPS, REQS, LOCAL), BF16), 0, (pieces, tokens_in))


def solution(mesh):
    fine = Mesh(mesh.devices.reshape(NH, NL, NX, NY, NC), SEQ + TP)
    cols = P(None, TP)
    rows = P(TP, None)
    cache = P(SEQ, TP, None)
    in_specs = (
        P(None, None, TP), P(), P(), cols, cols, cols, rows, cols, cols, rows,
        cache, cache, cache, cache, P(), P(),
    )
    return jax.shard_map(body, mesh=fine, in_specs=in_specs, out_specs=P(None, None, TP), check_vma=False)
```

```python
import math

import jax
import jax.numpy as jnp
import numpy as np
from jax import lax
from jax.experimental import pallas as pl
from jax.experimental.pallas import tpu as pltpu
from jax.sharding import Mesh, PartitionSpec as P

HEADS = 32
KV_HEADS = 8
GROUP = HEADS // KV_HEADS
HD = 80
HALF = HD // 2
D = 2560
WIN = 4096
STEPS = 8
REQS = 4
ROWS = STEPS * REQS
NY, NC = 4, 2
SEQ_SIZES = {"zh": 4, "zl": 2, "xh": 2, "xl": 2}
SEQ = tuple(SEQ_SIZES)
TEAM = ('zl', 'xh', 'xl')
NG = math.prod(SEQ_SIZES[a] for a in TEAM)
TOK = STEPS * REQS // NG
NSEQ = math.prod(SEQ_SIZES.values())
NTP = NY * NC
LOCAL = D // NTP
SLOTS = WIN // NSEQ
SSLOTS = 16
EPS = 1e-05
MASKED = -1e30
TP = ("y", "c")
F32 = jnp.float32
BF16 = jnp.bfloat16
NN = (((1,), (0,)), ((), ()))
NT = (((1,), (1,)), ((), ()))
TN = (((0,), (0,)), ((), ()))


def mm(a, b, dims):
    return lax.dot_general(a, b, dims, preferred_element_type=F32)


def iota(shape, dim):
    return lax.broadcasted_iota(jnp.int32, shape, dim)


def wide_rows(piece):
    return jnp.concatenate([piece(c) for c in range(NTP)], axis=-1)


def rank_in(axes):
    rank = 0
    for a in axes:
        rank = rank * SEQ_SIZES[a] + lax.axis_index(a)
    return rank


def team_of(seq_rank):
    at = dict(zip(SEQ, np.unravel_index(seq_rank, tuple(SEQ_SIZES.values()))))
    rank = 0
    for a in TEAM:
        rank = rank * SEQ_SIZES[a] + int(at[a])
    return rank


def split3(v):
    hi = v.astype(BF16).astype(F32)
    mid = (v - hi).astype(BF16).astype(F32)
    low = (v - hi - mid).astype(BF16).astype(F32)
    return hi, mid, low


def spread_kernel(tokens_ref, out_ref, after_ref):
    after_ref[...] = jnp.zeros(after_ref.shape, F32)
    rows = jnp.concatenate([tokens_ref[t].astype(F32) for t in range(STEPS)], axis=0)
    packed = jnp.concatenate(
        [rows[:, :128], rows[:, 128:256], jnp.concatenate([rows[: ROWS // 2, 256:], rows[ROWS // 2 :, 256:]], axis=1)], axis=0
    ).astype(BF16)
    for to in range(NTP):
        out_ref[to] = packed


def unpack_rows(packed):
    last = packed[2 * ROWS :]
    tail = jnp.concatenate([last[:, :64], last[:, 64:]], axis=0)
    return jnp.concatenate([packed[:ROWS], packed[ROWS : 2 * ROWS], tail], axis=1)


def finish_kernel(piece_ref, tokens_ref, out_ref):
    for team in range(NG):
        total = jnp.sum(piece_ref[team * NTP : (team + 1) * NTP].astype(F32), axis=0)
        rows = [
            jnp.concatenate([total[2 * p], total[2 * p + 1], total[4][:, 64 * p : 64 * p + 64]], axis=1) for p in range(2)
        ]
        out_ref[team] = (tokens_ref[team].astype(F32) + jnp.concatenate(rows, axis=0)).astype(BF16)


def table_kernel(
    after_ref, seen_hbm, len_hbm, freq_ref, cos_ref, sin_ref, hide_long_ref, hide_short_ref, hide_new_ref, seen_ref, len_ref, sems,
):
    loads = [pltpu.make_async_copy(seen_hbm, seen_ref, sems.at[0]), pltpu.make_async_copy(len_hbm, len_ref, sems.at[1])]
    for load in loads:
        load.start()
    for load in loads:
        load.wait()
    seq_rank = rank_in(SEQ)

    def cached(req):
        return jnp.where(req == 1, len_ref[0], jnp.where(req == 2, len_ref[1], len_ref[2]))

    col = iota((HALF, ROWS), 1)
    base = jnp.where((col & 3) == 0, seen_ref[0], cached(col & 3))
    angles = ((col >> 2) + base).astype(F32) * freq_ref[...]
    cos_ref[...] = jnp.cos(angles)
    sin_ref[...] = jnp.sin(angles)

    def row_ids(shape):
        row = iota(shape, 0)
        return row & 3, (row >> 2) & 7, iota(shape, 1)

    def hidden(see):
        return jnp.where(see, 0.0, MASKED)

    r, t, j = row_ids(hide_long_ref.shape)
    age = (seq_rank * SLOTS + j - seen_ref[0]) & (WIN - 1)
    hide_long_ref[...] = hidden((r == 0) & (age > t))
    r, t, j = row_ids(hide_short_ref.shape)
    hide_short_ref[...] = hidden(((j >> 4) + 1 == r) & (seq_rank * SSLOTS + (j & 15) < cached(r)))
    r, t, j = row_ids(hide_new_ref.shape)
    hide_new_ref[...] = hidden(((j & 3) == r) & ((j >> 2) <= t) & (seq_rank == 0))


def attend_kernel(
    x_ref, gain_ref, cos_ref, sin_ref, hide_long_ref, hide_short_ref, hide_new_ref, wq_ref, wk_ref, wv_ref,
    lk_ref, lv_ref, sk_ref, sv_ref, part_ref, own_ref,
):
    team_rank = rank_in(TEAM)
    x_bf = wide_rows(lambda c: unpack_rows(x_ref[c]))
    x = x_bf.astype(F32)
    mean_square = jnp.mean(x * x, axis=-1, keepdims=True)
    normed = (x * lax.rsqrt(mean_square + EPS) * gain_ref[...].astype(F32).reshape(1, D)).astype(BF16)
    pick = (iota((8, ROWS), 1) == team_rank * TOK + iota((8, ROWS), 0)).astype(BF16)
    own_ref[...] = mm(pick, x_bf, NN)[:TOK]

    cos = cos_ref[...]
    sin = sin_ref[...]

    def rope(v):
        front, back = v[:HALF], v[HALF:]
        return jnp.concatenate([front * cos - back * sin, back * cos + front * sin], axis=0)

    q_t = mm(wq_ref[...], normed, NT)
    k_t = rope(mm(wk_ref[...], normed, NT)).astype(BF16)
    v_t = mm(wv_ref[...], normed, NT).astype(BF16)
    q_all = jnp.concatenate([rope(q_t[h * HD : (h + 1) * HD]) for h in range(GROUP)], axis=1)
    q = q_all.T.astype(BF16)

    scale = 1.0 / math.sqrt(HD)
    n_rows = GROUP * ROWS
    sk = jnp.concatenate([sk_ref[:, r * HD : (r + 1) * HD] for r in range(REQS - 1)], axis=0)
    sv = jnp.concatenate([sv_ref[:, r * HD : (r + 1) * HD] for r in range(REQS - 1)], axis=0)

    def scores(raw, hide_ref):
        hide = hide_ref[...]
        return jnp.where(hide < 0.0, MASKED, raw * scale), hide

    s_long, hide_long = scores(mm(q, lk_ref[...], NN), hide_long_ref)
    s_short, hide_short = scores(mm(q, sk, NT), hide_short_ref)
    s_new, hide_new = scores(mm(q, k_t, NN), hide_new_ref)
    top = jnp.maximum(
        jnp.maximum(jnp.max(s_long, axis=-1, keepdims=True), jnp.max(s_short, axis=-1, keepdims=True)),
        jnp.max(s_new, axis=-1, keepdims=True),
    )
    w_long = jnp.where(hide_long < 0.0, 0.0, jnp.exp(s_long - top))
    w_short = jnp.where(hide_short < 0.0, 0.0, jnp.exp(s_short - top))
    w_new = jnp.where(hide_new < 0.0, 0.0, jnp.exp(s_new - top))
    total = (
        jnp.sum(w_long, axis=-1, keepdims=True)
        + jnp.sum(w_short, axis=-1, keepdims=True)
        + jnp.sum(w_new, axis=-1, keepdims=True)
    )
    acc = (
        mm(w_long.astype(BF16), lv_ref[...], NT)
        + mm(w_short.astype(BF16), sv, NN)
        + mm(w_new.astype(BF16), v_t, NT)
    )
    top_a, top_b, top_c = split3(top)
    sum_a, sum_b, _ = split3(total)
    acc = jnp.concatenate([acc, jnp.zeros((n_rows, 128 - HD), F32)], axis=1)
    lane = iota(acc.shape, 1)
    for k, v in enumerate((top_a, top_b, top_c, sum_a, sum_b)):
        acc = jnp.where(lane == HD + k, v, acc)
    for team in range(NG):
        rows = jnp.concatenate(
            [acc[h * ROWS + team * TOK : h * ROWS + (team + 1) * TOK] for h in range(GROUP)], axis=0
        ).astype(BF16)
        for to in range(NSEQ):
            if team_of(to) == team:
                part_ref[to] = rows


def combine_kernel(part_ref, wo_ref, out_ref):
    part = part_ref[...]
    src = iota((128, 256), 0)
    dst = iota((128, 256), 1)
    spread = (
        ((dst < 128) & (src >= HD) & (src < HD + 3)) | ((dst >= 128) & (src >= HD + 3) & (src < HD + 5))
    ).astype(BF16)
    stats = mm(part.reshape(NSEQ * GROUP * TOK, 128), spread, NN)
    top = stats[:, :128].reshape(NSEQ, GROUP * TOK, 128)
    total = stats[:, 128:].reshape(NSEQ, GROUP * TOK, 128)
    factor = jnp.exp(top - jnp.max(top, axis=0, keepdims=True))
    weighted = jnp.sum(part.astype(F32) * factor, axis=0)
    attended = weighted / jnp.sum(total * factor, axis=0)
    attended = jnp.concatenate([attended[h * TOK : (h + 1) * TOK, :HD] for h in range(GROUP)], axis=1)
    term = mm(attended.astype(BF16), wo_ref[...], NN).astype(BF16)
    for to in range(NTP):
        out_ref[to] = term


def mlp_kernel(part_ref, own_ref, gain_ref, wg_ref, wu_ref, wd_ref, out_ref):
    tp_rank = lax.axis_index("y") * NC + lax.axis_index("c")
    head_sum = jnp.sum(part_ref[...].astype(F32), axis=0)
    stream = own_ref[...] + head_sum
    mean_square = jnp.mean(stream * stream, axis=-1, keepdims=True)
    mlp_in = stream * lax.rsqrt(mean_square + EPS) * gain_ref[...].astype(F32).reshape(1, D)
    mlp_in = jnp.concatenate([mlp_in, jnp.zeros((16 - TOK, D), F32)], axis=0).astype(BF16)
    gate = mm(wg_ref[...], mlp_in, NT)
    up = mm(wu_ref[...], mlp_in, NT)
    hidden = (gate / (1.0 + jnp.exp(-gate)) * up).astype(BF16)
    down = mm(hidden, wd_ref[...], TN)[:TOK]
    for to in range(NTP):
        cols = slice(to * LOCAL, (to + 1) * LOCAL)
        piece = (down[:, cols] + jnp.where(tp_rank == to, head_sum[:, cols], 0.0)).astype(BF16)
        tiles = [piece[p : p + 2, k : k + 128] for p in (0, 2) for k in (0, 128)]
        tiles.append(jnp.concatenate([piece[:2, 256:], piece[2:, 256:]], axis=1))
        for g_to in range(NG):
            for k, tile in enumerate(tiles):
                out_ref[g_to * NTP + to, k] = tile


def call(kernel, out_shape, args, scratch=(), in_hbm=()):
    specs = [pl.BlockSpec(memory_space=pltpu.HBM if i in in_hbm else pltpu.VMEM) for i in range(len(args))]
    return pl.pallas_call(
        kernel,
        out_shape=out_shape,
        in_specs=specs,
        scratch_shapes=scratch,
        cost_estimate=pl.CostEstimate(flops=50_000_000_000, bytes_accessed=100_000_000, transcendentals=0),
        compiler_params=pltpu.CompilerParams(vmem_limit_bytes=16 * 1024 * 1024),
    )(*args)


def body(
    tokens_in, attn_gain, mlp_gain, proj_query, proj_key, proj_value, proj_out, proj_gate, proj_up,
    proj_down, long_keys, long_values, short_keys, short_values, long_seen, short_len,
):
    freq = 10000.0 ** (-2.0 * np.arange(HALF) / HD)
    freq = jnp.asarray(np.repeat(freq[:, None], ROWS, axis=1).astype(np.float32))
    def f32_of(*dims):
        return jax.ShapeDtypeStruct(dims, F32)

    copies, after = call(spread_kernel, (jax.ShapeDtypeStruct((NTP, ROWS * LOCAL // 128, 128), BF16), f32_of(8, 128)), (tokens_in,))
    n_rows = GROUP * ROWS
    tables = call(
        table_kernel,
        (f32_of(HALF, ROWS), f32_of(HALF, ROWS), f32_of(n_rows, SLOTS), f32_of(n_rows, 3 * SSLOTS), f32_of(n_rows, ROWS)),
        (after, long_seen, short_len, freq),
        (pltpu.SMEM((1,), jnp.int32), pltpu.SMEM((3,), jnp.int32), pltpu.SemaphoreType.DMA((2,))),
        {1, 2},
    )
    x_all = lax.all_to_all(copies, TP, 0, 0, tiled=True)
    parts, own = call(
        attend_kernel,
        (jax.ShapeDtypeStruct((NSEQ, GROUP * TOK, 128), BF16), jax.ShapeDtypeStruct((TOK, D), F32)),
        (
            x_all, attn_gain, *tables,
            proj_query.T, proj_key.T, proj_value.T,
            long_keys.reshape(SLOTS, HD).T, long_values.reshape(SLOTS, HD).T,
            short_keys.reshape(SSLOTS, 3 * HD), short_values.reshape(SSLOTS, 3 * HD),
        ),
    )
    parts = lax.all_to_all(parts, SEQ, 0, 0, tiled=True)
    terms = call(combine_kernel, jax.ShapeDtypeStruct((NTP, TOK, D), BF16), (parts, proj_out))
    terms = lax.all_to_all(terms, TP, 0, 0, tiled=True)
    pieces = call(
        mlp_kernel,
        jax.ShapeDtypeStruct((NG * NTP, 5, 2, 128), BF16),
        (terms, own, mlp_gain, proj_gate.T, proj_up.T, proj_down),
    )
    pieces = lax.all_to_all(pieces, TEAM + TP, 0, 0, tiled=True)
    return call(finish_kernel, jax.ShapeDtypeStruct((STEPS, REQS, LOCAL), BF16), (pieces, tokens_in))


def solution(mesh):
    fine = Mesh(mesh.devices.reshape(tuple(SEQ_SIZES.values()) + (NY, NC)), SEQ + TP)
    cols = P(None, TP)
    rows = P(TP, None)
    cache = P(SEQ, TP, None)
    in_specs = (
        P(None, None, TP), P(), P(), cols, cols, cols, rows, cols, cols, rows,
        cache, cache, cache, cache, P(), P(),
    )
    return jax.shard_map(body, mesh=fine, in_specs=in_specs, out_specs=P(None, None, TP), check_vma=False)
```

```python
import math

import jax
import jax.numpy as jnp
import numpy as np
from jax import lax
from jax.experimental import pallas as pl
from jax.experimental.pallas import tpu as pltpu
from jax.sharding import Mesh, PartitionSpec as P

HEADS = 32
KV_HEADS = 8
GROUP = HEADS // KV_HEADS
HD = 80
HALF = HD // 2
D = 2560
WIN = 4096
STEPS = 8
REQS = 4
ROWS = STEPS * REQS
NY, NC = 4, 2
SEQ_SIZES = {"zh": 4, "zl": 2, "xh": 2, "xl": 2}
SEQ = tuple(SEQ_SIZES)
TEAM = ('zl', 'xh', 'xl')
NG = math.prod(SEQ_SIZES[a] for a in TEAM)
TOK = STEPS * REQS // NG
NSEQ = math.prod(SEQ_SIZES.values())
NTP = NY * NC
LOCAL = D // NTP
SLOTS = WIN // NSEQ
SSLOTS = 16
HELD = SLOTS + 3 * SSLOTS
EPS = 1e-05
MASKED = -1e30
TP = ("y", "c")
F32 = jnp.float32
BF16 = jnp.bfloat16
NN = (((1,), (0,)), ((), ()))
NT = (((1,), (1,)), ((), ()))
TN = (((0,), (0,)), ((), ()))


def mm(a, b, dims):
    return lax.dot_general(a, b, dims, preferred_element_type=F32)


def iota(shape, dim):
    return lax.broadcasted_iota(jnp.int32, shape, dim)


def wide_rows(piece):
    return jnp.concatenate([piece(c) for c in range(NTP)], axis=-1)


def rank_in(axes):
    rank = 0
    for a in axes:
        rank = rank * SEQ_SIZES[a] + lax.axis_index(a)
    return rank


def team_of(seq_rank):
    at = dict(zip(SEQ, np.unravel_index(seq_rank, tuple(SEQ_SIZES.values()))))
    rank = 0
    for a in TEAM:
        rank = rank * SEQ_SIZES[a] + int(at[a])
    return rank


def split3(v):
    hi = v.astype(BF16).astype(F32)
    mid = (v - hi).astype(BF16).astype(F32)
    low = (v - hi - mid).astype(BF16).astype(F32)
    return hi, mid, low


def spread_kernel(tokens_ref, out_ref, after_ref):
    after_ref[...] = jnp.zeros(after_ref.shape, F32)
    rows = jnp.concatenate([tokens_ref[t].astype(F32) for t in range(STEPS)], axis=0)
    packed = jnp.concatenate(
        [rows[:, :128], rows[:, 128:256], jnp.concatenate([rows[: ROWS // 2, 256:], rows[ROWS // 2 :, 256:]], axis=1)], axis=0
    ).astype(BF16)
    for to in range(NTP):
        out_ref[to] = packed


def unpack_rows(packed):
    last = packed[2 * ROWS :]
    tail = jnp.concatenate([last[:, :64], last[:, 64:]], axis=0)
    return jnp.concatenate([packed[:ROWS], packed[ROWS : 2 * ROWS], tail], axis=1)


def finish_kernel(piece_ref, tokens_ref, out_ref):
    for team in range(NG):
        total = jnp.sum(piece_ref[team * NTP : (team + 1) * NTP].astype(F32), axis=0)
        rows = [
            jnp.concatenate([total[2 * p], total[2 * p + 1], total[4][:, 64 * p : 64 * p + 64]], axis=1) for p in range(2)
        ]
        out_ref[team] = (tokens_ref[team].astype(F32) + jnp.concatenate(rows, axis=0)).astype(BF16)


def table_kernel(
    after_ref, seen_hbm, len_hbm, freq_ref, lk_ref, lv_ref, sk_ref, sv_ref,
    cos_ref, sin_ref, hide_ref, keys_ref, values_ref, seen_ref, len_ref, sems,
):
    loads = [pltpu.make_async_copy(seen_hbm, seen_ref, sems.at[0]), pltpu.make_async_copy(len_hbm, len_ref, sems.at[1])]
    for load in loads:
        load.start()
    for load in loads:
        load.wait()
    seq_rank = rank_in(SEQ)

    def cached(req):
        return jnp.where(req == 1, len_ref[0], jnp.where(req == 2, len_ref[1], len_ref[2]))

    col = iota((HALF, ROWS), 1)
    base = jnp.where((col & 3) == 0, seen_ref[0], cached(col & 3))
    angles = ((col >> 2) + base).astype(F32) * freq_ref[...]
    cos_ref[...] = jnp.cos(angles)
    sin_ref[...] = jnp.sin(angles)

    def hide(first, count, see):
        shape = (count, GROUP * ROWS)
        lane = iota(shape, 1)
        hide_ref[first : first + count] = jnp.where(see(lane & 3, (lane >> 2) & 7, iota(shape, 0)), 0.0, MASKED)

    hide(0, SLOTS, lambda r, t, j: (r == 0) & (((seq_rank * SLOTS + j - seen_ref[0]) & (WIN - 1)) > t))
    hide(SLOTS, 3 * SSLOTS, lambda r, t, j: ((j >> 4) + 1 == r) & (seq_rank * SSLOTS + (j & 15) < cached(r)))
    hide(HELD, ROWS, lambda r, t, j: ((j & 3) == r) & ((j >> 2) <= t) & (seq_rank == 0))
    keys_ref[:SLOTS] = lk_ref[...].astype(F32).T.astype(BF16)
    for req in range(REQS - 1):
        cols = slice(req * HD, (req + 1) * HD)
        keys_ref[SLOTS + req * SSLOTS : SLOTS + (req + 1) * SSLOTS] = sk_ref[:, cols]
    short = jnp.concatenate([sv_ref[:, r * HD : (r + 1) * HD].astype(F32) for r in range(REQS - 1)], axis=0)
    values_ref[...] = jnp.concatenate([lv_ref[...].astype(F32), short.T], axis=1).astype(BF16)


def attend_kernel(
    x_ref, gain_ref, cos_ref, sin_ref, hide_ref, keys_ref, values_ref, wq_ref, wk_ref, wv_ref, part_ref, own_ref,
):
    team_rank = rank_in(TEAM)
    x_bf = wide_rows(lambda c: unpack_rows(x_ref[c]))
    x = x_bf.astype(F32)
    mean_square = jnp.mean(x * x, axis=-1, keepdims=True)
    normed = (x * lax.rsqrt(mean_square + EPS) * gain_ref[...].astype(F32).reshape(1, D)).astype(BF16)
    pick = (iota((8, ROWS), 1) == team_rank * TOK + iota((8, ROWS), 0)).astype(BF16)
    own_ref[...] = mm(pick, x_bf, NN)[:TOK]

    cos = cos_ref[...]
    sin = sin_ref[...]

    def rope(v):
        front, back = v[:HALF], v[HALF:]
        return jnp.concatenate([front * cos - back * sin, back * cos + front * sin], axis=0)

    k_new = rope(mm(wk_ref[...], normed, NT)).T.astype(BF16)
    v_new = mm(wv_ref[...], normed, NT).astype(BF16)
    q_t = mm(normed, wq_ref[...], NT).T
    q = jnp.concatenate([rope(q_t[h * HD : (h + 1) * HD]) for h in range(GROUP)], axis=1).astype(BF16)

    seen = hide_ref[...] == 0.0
    scores = mm(jnp.concatenate([keys_ref[...], k_new], axis=0), q, NN) * (1.0 / math.sqrt(HD))
    scores = jnp.where(seen, scores, MASKED)
    top = jnp.max(scores, axis=0, keepdims=True)
    weights = jnp.where(seen, jnp.exp(scores - top), 0.0)
    total = jnp.sum(weights, axis=0, keepdims=True)
    weights = weights.astype(BF16)
    acc = mm(values_ref[...], weights[:HELD], NN) + mm(v_new, weights[HELD:], NN)
    some = total > 0.0
    level = jnp.where(some, top + jnp.log(jnp.where(some, total, 1.0)), MASKED)
    filler = jnp.zeros((128 - HD - 3, GROUP * ROWS), F32)
    acc = jnp.concatenate([acc * (1.0 / jnp.where(some, total, 1.0)), *split3(level), filler], axis=0).T
    for team in range(NG):
        rows = jnp.concatenate(
            [acc[h * ROWS + team * TOK : h * ROWS + (team + 1) * TOK] for h in range(GROUP)], axis=0
        ).astype(BF16)
        for to in range(NSEQ):
            if team_of(to) == team:
                part_ref[to] = rows


def combine_kernel(part_ref, wo_ref, out_ref):
    part = part_ref[...]
    src = iota((128, 128), 0)
    spread = ((src >= HD) & (src < HD + 3)).astype(BF16)
    level = mm(part.reshape(NSEQ * GROUP * TOK, 128), spread, NN).reshape(NSEQ, GROUP * TOK, 128)
    factor = jnp.exp(level - jnp.max(level, axis=0, keepdims=True))
    attended = jnp.sum(part.astype(F32) * factor, axis=0) / jnp.sum(factor, axis=0)
    attended = jnp.concatenate([attended[h * TOK : (h + 1) * TOK, :HD] for h in range(GROUP)], axis=1)
    term = mm(attended.astype(BF16), wo_ref[...], NN).astype(BF16)
    for to in range(NTP):
        out_ref[to] = term


def mlp_kernel(part_ref, own_ref, gain_ref, wg_ref, wu_ref, wd_ref, out_ref):
    tp_rank = lax.axis_index("y") * NC + lax.axis_index("c")
    head_sum = jnp.sum(part_ref[...].astype(F32), axis=0)
    stream = own_ref[...] + head_sum
    mean_square = jnp.mean(stream * stream, axis=-1, keepdims=True)
    mlp_in = stream * lax.rsqrt(mean_square + EPS) * gain_ref[...].astype(F32).reshape(1, D)
    mlp_in = jnp.concatenate([mlp_in, jnp.zeros((16 - TOK, D), F32)], axis=0).astype(BF16)
    gate = mm(mlp_in, wg_ref[...], NT)
    up = mm(mlp_in, wu_ref[...], NT)
    hidden = (gate / (1.0 + jnp.exp(-gate)) * up).astype(BF16)
    down = mm(hidden, wd_ref[...], NN)[:TOK]
    for to in range(NTP):
        cols = slice(to * LOCAL, (to + 1) * LOCAL)
        piece = (down[:, cols] + jnp.where(tp_rank == to, head_sum[:, cols], 0.0)).astype(BF16)
        tiles = [piece[p : p + 2, k : k + 128] for p in (0, 2) for k in (0, 128)]
        tiles.append(jnp.concatenate([piece[:2, 256:], piece[2:, 256:]], axis=1))
        for g_to in range(NG):
            for k, tile in enumerate(tiles):
                out_ref[g_to * NTP + to, k] = tile


def call(kernel, out_shape, args, scratch=(), in_hbm=()):
    specs = [pl.BlockSpec(memory_space=pltpu.HBM if i in in_hbm else pltpu.VMEM) for i in range(len(args))]
    return pl.pallas_call(
        kernel,
        out_shape=out_shape,
        in_specs=specs,
        scratch_shapes=scratch,
        cost_estimate=pl.CostEstimate(flops=50_000_000_000, bytes_accessed=100_000_000, transcendentals=0),
        compiler_params=pltpu.CompilerParams(vmem_limit_bytes=16 * 1024 * 1024),
    )(*args)


def body(
    tokens_in, attn_gain, mlp_gain, proj_query, proj_key, proj_value, proj_out, proj_gate, proj_up,
    proj_down, long_keys, long_values, short_keys, short_values, long_seen, short_len,
):
    freq = 10000.0 ** (-2.0 * np.arange(HALF) / HD)
    freq = jnp.asarray(np.repeat(freq[:, None], ROWS, axis=1).astype(np.float32))
    def f32_of(*dims):
        return jax.ShapeDtypeStruct(dims, F32)

    copies, after = call(spread_kernel, (jax.ShapeDtypeStruct((NTP, ROWS * LOCAL // 128, 128), BF16), f32_of(8, 128)), (tokens_in,))
    n_rows = GROUP * ROWS
    tables = call(
        table_kernel,
        (
            f32_of(HALF, ROWS), f32_of(HALF, ROWS), f32_of(HELD + ROWS, n_rows),
            jax.ShapeDtypeStruct((HELD, HD), BF16), jax.ShapeDtypeStruct((HD, HELD), BF16),
        ),
        (
            after, long_seen, short_len, freq,
            long_keys.reshape(SLOTS, HD).T, long_values.reshape(SLOTS, HD).T,
            short_keys.reshape(SSLOTS, 3 * HD), short_values.reshape(SSLOTS, 3 * HD),
        ),
        (pltpu.SMEM((1,), jnp.int32), pltpu.SMEM((3,), jnp.int32), pltpu.SemaphoreType.DMA((2,))),
        {1, 2},
    )
    x_all = lax.all_to_all(copies, TP, 0, 0, tiled=True)
    parts, own = call(
        attend_kernel,
        (jax.ShapeDtypeStruct((NSEQ, GROUP * TOK, 128), BF16), jax.ShapeDtypeStruct((TOK, D), F32)),
        (
            x_all, attn_gain, *tables, proj_query.T, proj_key.T, proj_value.T,
        ),
    )
    parts = lax.all_to_all(parts, SEQ, 0, 0, tiled=True)
    terms = call(combine_kernel, jax.ShapeDtypeStruct((NTP, TOK, D), BF16), (parts, proj_out))
    terms = lax.all_to_all(terms, TP, 0, 0, tiled=True)
    pieces = call(
        mlp_kernel,
        jax.ShapeDtypeStruct((NG * NTP, 5, 2, 128), BF16),
        (terms, own, mlp_gain, proj_gate.T, proj_up.T, proj_down),
    )
    pieces = lax.all_to_all(pieces, TEAM + TP, 0, 0, tiled=True)
    return call(finish_kernel, jax.ShapeDtypeStruct((STEPS, REQS, LOCAL), BF16), (pieces, tokens_in))


def solution(mesh):
    fine = Mesh(mesh.devices.reshape(tuple(SEQ_SIZES.values()) + (NY, NC)), SEQ + TP)
    cols = P(None, TP)
    rows = P(TP, None)
    cache = P(SEQ, TP, None)
    in_specs = (
        P(None, None, TP), P(), P(), cols, cols, cols, rows, cols, cols, rows,
        cache, cache, cache, cache, P(), P(),
    )
    return jax.shard_map(body, mesh=fine, in_specs=in_specs, out_specs=P(None, None, TP), check_vma=False)
```

```python
import math

import jax
import jax.numpy as jnp
import numpy as np
from jax import lax
from jax.experimental import pallas as pl
from jax.experimental.pallas import tpu as pltpu
from jax.sharding import Mesh, PartitionSpec as P

HEADS = 32
KV_HEADS = 8
GROUP = HEADS // KV_HEADS
HD = 80
HALF = HD // 2
D = 2560
WIN = 4096
STEPS = 8
REQS = 4
ROWS = STEPS * REQS
NY, NC = 4, 2
SEQ_SIZES = {"zh": 4, "zl": 2, "xh": 2, "xl": 2}
SEQ = tuple(SEQ_SIZES)
TEAM = ('zl', 'xh', 'xl')
NG = math.prod(SEQ_SIZES[a] for a in TEAM)
TOK = STEPS * REQS // NG
NSEQ = math.prod(SEQ_SIZES.values())
NTP = NY * NC
LOCAL = D // NTP
SLOTS = WIN // NSEQ
SSLOTS = 16
HELD = SLOTS + 3 * SSLOTS
WIDE = 384
EPS = 1e-05
MASKED = -1e30
TP = ("y", "c")
F32 = jnp.float32
BF16 = jnp.bfloat16
NN = (((1,), (0,)), ((), ()))
NT = (((1,), (1,)), ((), ()))
TN = (((0,), (0,)), ((), ()))


def mm(a, b, dims):
    return lax.dot_general(a, b, dims, preferred_element_type=F32)


def iota(shape, dim):
    return lax.broadcasted_iota(jnp.int32, shape, dim)


def wide_rows(piece):
    return jnp.concatenate([piece(c) for c in range(NTP)], axis=-1)


def rank_in(axes):
    rank = 0
    for a in axes:
        rank = rank * SEQ_SIZES[a] + lax.axis_index(a)
    return rank


def team_of(seq_rank):
    at = dict(zip(SEQ, np.unravel_index(seq_rank, tuple(SEQ_SIZES.values()))))
    rank = 0
    for a in TEAM:
        rank = rank * SEQ_SIZES[a] + int(at[a])
    return rank


def split3(v):
    hi = v.astype(BF16).astype(F32)
    mid = (v - hi).astype(BF16).astype(F32)
    low = (v - hi - mid).astype(BF16).astype(F32)
    return hi, mid, low


def spread_kernel(tokens_ref, out_ref, after_ref):
    after_ref[...] = jnp.zeros(after_ref.shape, F32)
    rows = jnp.concatenate([tokens_ref[t].astype(F32) for t in range(STEPS)], axis=0)
    packed = jnp.concatenate(
        [rows[:, :128], rows[:, 128:256], jnp.concatenate([rows[: ROWS // 2, 256:], rows[ROWS // 2 :, 256:]], axis=1)], axis=0
    ).astype(BF16)
    for to in range(NTP):
        out_ref[to] = packed


def unpack_rows(packed):
    last = packed[2 * ROWS :]
    tail = jnp.concatenate([last[:, :64], last[:, 64:]], axis=0)
    return jnp.concatenate([packed[:ROWS], packed[ROWS : 2 * ROWS], tail], axis=1)


def finish_kernel(piece_ref, tokens_ref, out_ref):
    for team in range(NG):
        total = jnp.sum(piece_ref[team * NTP : (team + 1) * NTP].astype(F32), axis=0)
        rows = [
            jnp.concatenate([total[2 * p], total[2 * p + 1], total[4][:, 64 * p : 64 * p + 64]], axis=1) for p in range(2)
        ]
        out_ref[team] = (tokens_ref[team].astype(F32) + jnp.concatenate(rows, axis=0)).astype(BF16)


def table_kernel(
    after_ref, seen_hbm, len_hbm, freq_ref, lk_ref, lv_ref, sk_ref, sv_ref,
    cos_ref, sin_ref, hide_ref, keys_ref, values_ref, seen_ref, len_ref, sems,
):
    loads = [pltpu.make_async_copy(seen_hbm, seen_ref, sems.at[0]), pltpu.make_async_copy(len_hbm, len_ref, sems.at[1])]
    for load in loads:
        load.start()
    for load in loads:
        load.wait()
    seq_rank = rank_in(SEQ)

    def cached(req):
        return jnp.where(req == 1, len_ref[0], jnp.where(req == 2, len_ref[1], len_ref[2]))

    col = iota((HALF, ROWS), 1)
    base = jnp.where((col & 3) == 0, seen_ref[0], cached(col & 3))
    angles = ((col >> 2) + base).astype(F32) * freq_ref[...]
    cos_ref[...] = jnp.cos(angles)
    sin_ref[...] = jnp.sin(angles)

    def hide(first, count, see):
        shape = (count, GROUP * ROWS)
        lane = iota(shape, 1)
        hide_ref[first : first + count] = jnp.where(see(lane & 3, (lane >> 2) & 7, iota(shape, 0)), 0.0, MASKED)

    hide(0, SLOTS, lambda r, t, j: (r == 0) & (((seq_rank * SLOTS + j - seen_ref[0]) & (WIN - 1)) > t))
    hide(SLOTS, 3 * SSLOTS, lambda r, t, j: ((j >> 4) + 1 == r) & (seq_rank * SSLOTS + (j & 15) < cached(r)))
    hide(HELD, ROWS, lambda r, t, j: ((j & 3) == r) & ((j >> 2) <= t) & (seq_rank == 0))
    keys_ref[:SLOTS] = lk_ref[...].astype(F32).T.astype(BF16)
    for req in range(REQS - 1):
        cols = slice(req * HD, (req + 1) * HD)
        keys_ref[SLOTS + req * SSLOTS : SLOTS + (req + 1) * SSLOTS] = sk_ref[:, cols]
    short = jnp.concatenate([sv_ref[:, r * HD : (r + 1) * HD].astype(F32) for r in range(REQS - 1)], axis=0)
    values_ref[...] = jnp.concatenate([lv_ref[...].astype(F32), short.T], axis=1).astype(BF16)


def attend_kernel(
    x_ref, gain_ref, cos_ref, sin_ref, hide_ref, keys_ref, values_ref, wq_ref, wk_ref, wv_ref, part_ref, own_ref,
):
    team_rank = rank_in(TEAM)
    x_bf = wide_rows(lambda c: unpack_rows(x_ref[c]))
    x = x_bf.astype(F32)
    mean_square = jnp.mean(x * x, axis=-1, keepdims=True)
    normed = (x * lax.rsqrt(mean_square + EPS) * gain_ref[...].astype(F32).reshape(1, D)).astype(BF16)
    pick = (iota((8, ROWS), 1) == team_rank * TOK + iota((8, ROWS), 0)).astype(BF16)
    own_ref[...] = mm(pick, x_bf, NN)[:TOK]

    cos = cos_ref[...]
    sin = sin_ref[...]

    def rope(v):
        front, back = v[:HALF], v[HALF:]
        return jnp.concatenate([front * cos - back * sin, back * cos + front * sin], axis=0)

    k_new = rope(mm(wk_ref[...], normed, NT)).T.astype(BF16)
    v_new = mm(wv_ref[...], normed, NT).astype(BF16)
    q_t = mm(wq_ref[...], normed, NT)
    q = jnp.concatenate([rope(q_t[h * HD : (h + 1) * HD]) for h in range(GROUP)], axis=1).astype(BF16)

    seen = hide_ref[...] == 0.0
    scores = mm(jnp.concatenate([keys_ref[...], k_new], axis=0), q, NN) * (1.0 / math.sqrt(HD))
    scores = jnp.where(seen, scores, MASKED)
    top = jnp.max(scores, axis=0, keepdims=True)
    weights = jnp.where(seen, jnp.exp(scores - top), 0.0)
    total = jnp.sum(weights, axis=0, keepdims=True)
    weights = weights.astype(BF16)
    acc = mm(values_ref[...], weights[:HELD], NN) + mm(v_new, weights[HELD:], NN)
    some = total > 0.0
    level = jnp.where(some, top + jnp.log(jnp.where(some, total, 1.0)), MASKED)
    filler = jnp.zeros((128 - HD - 3, GROUP * ROWS), F32)
    acc = jnp.concatenate([acc * (1.0 / jnp.where(some, total, 1.0)), *split3(level), filler], axis=0).T
    heads = [acc[h * ROWS : (h + 1) * ROWS] for h in range(GROUP)]
    packed = jnp.concatenate(
        [v[:, :HD] for v in heads] + [v[:, HD : HD + 3] for v in heads] + [jnp.zeros((ROWS, WIDE - GROUP * (HD + 3)), F32)],
        axis=1,
    )
    for team in range(NG):
        rows = packed[team * TOK : (team + 1) * TOK].astype(BF16)
        for to in range(NSEQ):
            if team_of(to) == team:
                part_ref[to] = rows


def combine_kernel(part_ref, wo_ref, out_ref):
    part = part_ref[...].astype(F32).reshape(NSEQ * TOK, WIDE)
    src = iota((WIDE, WIDE), 0) - GROUP * HD
    dst = iota((WIDE, WIDE), 1)
    spread = jnp.zeros((WIDE, WIDE), F32)
    for h in range(GROUP):
        at_head = (dst >= h * HD) & (dst < (h + 1) * HD) & (src >= 3 * h) & (src < 3 * h + 3)
        spread = jnp.where(at_head, 1.0, spread)
    level = mm(part.astype(BF16), spread.astype(BF16), NN).reshape(NSEQ * TOK // 8, 8, WIDE)
    top = jnp.max(level, axis=0)
    top = jnp.maximum(top, pltpu.roll(top, TOK, 0))
    factor = jnp.exp(level - top)
    weighted = jnp.sum(part.reshape(NSEQ * TOK // 8, 8, WIDE) * factor, axis=0)
    total = jnp.sum(factor, axis=0)
    attended = (weighted + pltpu.roll(weighted, TOK, 0)) / (total + pltpu.roll(total, TOK, 0))
    attended = attended[:TOK, : GROUP * HD]
    term = mm(attended.astype(BF16), wo_ref[...], NN).astype(BF16)
    for to in range(NTP):
        out_ref[to] = term


def mlp_kernel(part_ref, own_ref, gain_ref, wg_ref, wu_ref, wd_ref, out_ref):
    tp_rank = lax.axis_index("y") * NC + lax.axis_index("c")
    head_sum = jnp.sum(part_ref[...].astype(F32), axis=0)
    stream = own_ref[...] + head_sum
    mean_square = jnp.mean(stream * stream, axis=-1, keepdims=True)
    mlp_in = stream * lax.rsqrt(mean_square + EPS) * gain_ref[...].astype(F32).reshape(1, D)
    mlp_in = jnp.concatenate([mlp_in, jnp.zeros((16 - TOK, D), F32)], axis=0).astype(BF16)
    gate = mm(mlp_in, wg_ref[...], NT)
    up = mm(mlp_in, wu_ref[...], NT)
    hidden = (gate / (1.0 + jnp.exp(-gate)) * up).astype(BF16)
    down = mm(hidden, wd_ref[...], NN)[:TOK]
    for to in range(NTP):
        cols = slice(to * LOCAL, (to + 1) * LOCAL)
        piece = (down[:, cols] + jnp.where(tp_rank == to, head_sum[:, cols], 0.0)).astype(BF16)
        tiles = [piece[p : p + 2, k : k + 128] for p in (0, 2) for k in (0, 128)]
        tiles.append(jnp.concatenate([piece[:2, 256:], piece[2:, 256:]], axis=1))
        for g_to in range(NG):
            for k, tile in enumerate(tiles):
                out_ref[g_to * NTP + to, k] = tile


def call(kernel, out_shape, args, scratch=(), in_hbm=()):
    specs = [pl.BlockSpec(memory_space=pltpu.HBM if i in in_hbm else pltpu.VMEM) for i in range(len(args))]
    return pl.pallas_call(
        kernel,
        out_shape=out_shape,
        in_specs=specs,
        scratch_shapes=scratch,
        cost_estimate=pl.CostEstimate(flops=50_000_000_000, bytes_accessed=100_000_000, transcendentals=0),
        compiler_params=pltpu.CompilerParams(vmem_limit_bytes=16 * 1024 * 1024),
    )(*args)


def body(
    tokens_in, attn_gain, mlp_gain, proj_query, proj_key, proj_value, proj_out, proj_gate, proj_up,
    proj_down, long_keys, long_values, short_keys, short_values, long_seen, short_len,
):
    freq = 10000.0 ** (-2.0 * np.arange(HALF) / HD)
    freq = jnp.asarray(np.repeat(freq[:, None], ROWS, axis=1).astype(np.float32))
    def f32_of(*dims):
        return jax.ShapeDtypeStruct(dims, F32)

    copies, after = call(spread_kernel, (jax.ShapeDtypeStruct((NTP, ROWS * LOCAL // 128, 128), BF16), f32_of(8, 128)), (tokens_in,))
    n_rows = GROUP * ROWS
    tables = call(
        table_kernel,
        (
            f32_of(HALF, ROWS), f32_of(HALF, ROWS), f32_of(HELD + ROWS, n_rows),
            jax.ShapeDtypeStruct((HELD, HD), BF16), jax.ShapeDtypeStruct((HD, HELD), BF16),
        ),
        (
            after, long_seen, short_len, freq,
            long_keys.reshape(SLOTS, HD).T, long_values.reshape(SLOTS, HD).T,
            short_keys.reshape(SSLOTS, 3 * HD), short_values.reshape(SSLOTS, 3 * HD),
        ),
        (pltpu.SMEM((1,), jnp.int32), pltpu.SMEM((3,), jnp.int32), pltpu.SemaphoreType.DMA((2,))),
        {1, 2},
    )
    x_all = lax.all_to_all(copies, TP, 0, 0, tiled=True)
    parts, own = call(
        attend_kernel,
        (jax.ShapeDtypeStruct((NSEQ, TOK, WIDE), BF16), jax.ShapeDtypeStruct((TOK, D), F32)),
        (
            x_all, attn_gain, *tables, proj_query.T, proj_key.T, proj_value.T,
        ),
    )
    parts = lax.all_to_all(parts, SEQ, 0, 0, tiled=True)
    terms = call(combine_kernel, jax.ShapeDtypeStruct((NTP, TOK, D), BF16), (parts, proj_out))
    terms = lax.all_to_all(terms, TP, 0, 0, tiled=True)
    pieces = call(
        mlp_kernel,
        jax.ShapeDtypeStruct((NG * NTP, 5, 2, 128), BF16),
        (terms, own, mlp_gain, proj_gate.T, proj_up.T, proj_down),
    )
    pieces = lax.all_to_all(pieces, TEAM + TP, 0, 0, tiled=True)
    return call(finish_kernel, jax.ShapeDtypeStruct((STEPS, REQS, LOCAL), BF16), (pieces, tokens_in))


def solution(mesh):
    fine = Mesh(mesh.devices.reshape(tuple(SEQ_SIZES.values()) + (NY, NC)), SEQ + TP)
    cols = P(None, TP)
    rows = P(TP, None)
    cache = P(SEQ, TP, None)
    in_specs = (
        P(None, None, TP), P(), P(), cols, cols, cols, rows, cols, cols, rows,
        cache, cache, cache, cache, P(), P(),
    )
    return jax.shard_map(body, mesh=fine, in_specs=in_specs, out_specs=P(None, None, TP), check_vma=False)
```
